32 devices in a mesh: seq: 8 (over z, x), head: 4 (over y, core).
Axes of the slice: x: 2, y: 2, z: 4, core: 2. Of those that a mesh axis runs over, the one named last changes fastest.
Arguments:
- queries: bfloat16 [2, 8, 14336], P(None, 'seq', 'head'), may hold values from -150 to 150
- new_keys: bfloat16 [2, 8, 14336], P(None, 'seq', 'head'), may hold values from -6 to 6
- new_values: bfloat16 [2, 8, 14336], P(None, 'seq', 'head'), may hold values from -6 to 6
- cache_keys: bfloat16 [8192, 14336], P('seq', 'head'), may hold values from -6 to 6
- cache_values: bfloat16 [8192, 14336], P('seq', 'head'), may hold values from -6 to 6
- slopes: float32 [112], P('head'), may hold values from 7.324219e-05 to 0.025
- seg_blocks: int32 [8], replicated, may hold values from 1 to 32, 48 in all
- request_row: int32 [8], replicated, may hold values from 0 to 7, each once
- out_weight: bfloat16 [14336, 14336], P('head', 'seq'), may hold values from -0.046875 to 0.046875
- residual: bfloat16 [2, 8, 14336], P(None, 'head', 'seq'), may hold values from -6 to 6
Outputs:
- mixed: bfloat16 [2, 8, 14336], P(None, 'head', 'seq')
The draws below stay inside these ranges and needn't reach their ends.
Inputs may be any that keep to these rules, and one draw needn't show every extreme that they name: `seg_blocks`: the requests are packed in order from block 0; 48 blocks are used and the rest of the cache is unused. `request_row`: each query row belongs to exactly one request.
All inputs are finite; a program needn't handle non-finite values.
Results may differ from the reference program's by a relative error of at most 0.006.
Values may be sent and summed in bfloat16 or wider, within the bound.
A program may use at most 64 MiB of HBM per device.

```python
import math
import jax
import jax.numpy as jnp
import numpy as np
from jax import lax

HEADS = 112
HDIM = 128
D = 14336
BLK = 128
NBLK = 64
NCACHE = 8192
REQ = 8
MOST = 32
LIVE = 48


def draw_cache_keys(key, part):
    noise = jnp.clip(jax.random.normal(jax.random.fold_in(key, 11), (NCACHE, HEADS * HDIM), jnp.float32), -6.0, 6.0)
    return noise.astype(jnp.bfloat16)


def draw_queries(key, part):
    noise = jnp.clip(jax.random.normal(jax.random.fold_in(key, 13), (2, REQ, HEADS * HDIM), jnp.float32), -6.0, 6.0)
    return noise.astype(jnp.bfloat16)


def steps_of(key, extent, split, least, largest):
    gain, own = 1.0, jax.random.fold_in(key, 6)
    for dim, parts in split:
        steps = jnp.exp(jax.random.uniform(jax.random.fold_in(own, dim), (parts,), jnp.float32, least / len(split), largest / len(split)))
        gain = gain * jnp.repeat(steps, extent[dim] // parts).reshape([-1 if axis == dim else 1 for axis in range(len(extent))])
    return gain


def split_up(count, total, reach, lean):
    loads = [(1 << 20) // math.isqrt(rank ** lean) + 1 for rank in range(2, count + 1)]
    spare, holding = total - reach - (count - 1), [1] * (count - 1)
    while spare > 0:
        free = [i for i in range(count - 1) if holding[i] < reach]
        mass, left = sum([loads[i] for i in free]), spare
        for i in free:
            more = min(reach - holding[i], max(1, left * loads[i] // mass), spare)
            holding[i] = holding[i] + more
            spare = spare - more
    return np.array([reach] + holding)


def ragged(own_key, count, total, bound, slope):
    if count == 2:
        one = jax.random.randint(own_key, (), max(1, total - bound), min(bound, total - 1) + 1)
        return jnp.stack([one, total - one])
    lengths = jnp.asarray(split_up(count, total, bound, slope), jnp.int32)
    twos = (count - 1) // 2
    giver, receiver = lengths[1:1 + 2 * twos:2], lengths[2:2 + 2 * twos:2]
    slack = jnp.minimum(giver - 1, bound - receiver)
    moved = jax.random.randint(jax.random.fold_in(own_key, 1), (twos,), 0, 1 << 20) % (slack + 1)
    lengths = lengths.at[1:1 + 2 * twos:2].set(giver - moved).at[2:2 + 2 * twos:2].set(receiver + moved)
    return lengths[jax.random.permutation(jax.random.fold_in(own_key, 2), count)]


def centred(stream_key, dims, scale, bound, cuts=(), kind=jnp.bfloat16):
    drawn = scale * jax.random.normal(stream_key, dims, jnp.float32)
    if cuts:
        drawn = drawn * steps_of(stream_key, dims, cuts, -0.22, 0.18)
    return jnp.clip(drawn, -bound, bound).astype(kind)


def setup_inputs(seed: int = 0) -> dict:
    streams_of = jax.random.split(jax.random.key(seed), 11)
    queries = draw_queries(jax.random.fold_in(streams_of[10], 71), 0)
    new_keys = centred(streams_of[1], (2, REQ, HEADS * HDIM), 1.0, 6.0, ((1, 8), (2, 4)))
    new_values = centred(streams_of[2], (2, REQ, HEADS * HDIM), 1.0, 6.0, ((1, 8), (2, 4)))
    cache_keys = draw_cache_keys(jax.random.fold_in(streams_of[10], 71), 0)
    cache_values = centred(streams_of[4], (NCACHE, HEADS * HDIM), 1.0, 6.0, ((0, 8), (1, 4)))
    slopes = jnp.clip(jnp.exp(math.log(0.025) - 5.8328595 * jax.random.uniform(streams_of[5], (HEADS,), jnp.float32) ** steps_of(streams_of[5], (HEADS,), ((0, 4),), -0.2, 0.2)), 7.324219041038305e-05, 0.025)
    seg_blocks = ragged(streams_of[6], REQ, LIVE, MOST, 2).astype(jnp.int32)
    request_row = jax.random.permutation(streams_of[7], REQ).astype(jnp.int32)
    out_weight = centred(streams_of[8], (HEADS * HDIM, D), (HEADS * HDIM) ** -0.5, 0.046875, ((0, 4), (1, 8)))
    residual = centred(streams_of[9], (2, REQ, D), 1.0, 6.0, ((1, 4), (2, 8)))
    return dict(queries=queries, new_keys=new_keys, new_values=new_values, cache_keys=cache_keys, cache_values=cache_values, slopes=slopes, seg_blocks=seg_blocks, request_row=request_row, out_weight=out_weight, residual=residual)


NEG = -1e+30

def self_terms(q, k, v, slopes, scale):
    q = q.astype(jnp.float32)
    k = k.astype(jnp.float32)
    v = v.astype(jnp.float32)
    first = lax.optimization_barrier(jnp.sum(q[0] * k[0], axis=-1)) * scale
    cross = lax.optimization_barrier(jnp.sum(q[1] * k[0], axis=-1)) * scale - slopes
    second = lax.optimization_barrier(jnp.sum(q[1] * k[1], axis=-1)) * scale
    upper = jnp.maximum(cross, second)
    e_cross = jnp.exp(cross - upper)
    e_second = jnp.exp(second - upper)
    top = jnp.stack([first, upper])
    total = jnp.stack([jnp.ones_like(first), e_cross + e_second])
    acc = jnp.stack([v[0], e_cross[..., None] * v[0] + e_second[..., None] * v[1]])
    return (top, total, acc)

def reference(queries, new_keys, new_values, cache_keys, cache_values, slopes, seg_blocks, request_row, out_weight, residual):
    scale = 1.0 / math.sqrt(HDIM)
    starts = jnp.cumsum(seg_blocks) - seg_blocks
    index = jnp.arange(NBLK, dtype=jnp.int32)
    hit = (index[:, None] >= starts[None, :]) & (index[:, None] < (starts + seg_blocks)[None, :])
    live = jnp.any(hit, axis=1)
    block_row = lax.optimization_barrier(jnp.sum(jnp.where(hit, request_row[None, :], 0), axis=1)).astype(jnp.int32)
    first = lax.optimization_barrier(jnp.sum(jnp.where(hit, starts[None, :], 0), axis=1)).astype(jnp.int32)
    length = lax.optimization_barrier(jnp.sum(jnp.where(hit, seg_blocks[None, :], 0), axis=1)).astype(jnp.int32)
    base = (length * BLK - (index - first) * BLK).astype(jnp.int32)
    block_query = jnp.take(queries, block_row, axis=1).reshape(2, NBLK, HEADS, HDIM).transpose(1, 0, 2, 3)
    keys = cache_keys.reshape(NBLK, BLK, HEADS, HDIM)
    values = cache_values.reshape(NBLK, BLK, HEADS, HDIM)

    def block_term(args):
        keys_b, values_b, query_b, base_b, live_b = args
        scores = jnp.einsum('shd,thd->sht', query_b.astype(jnp.float32), keys_b.astype(jnp.float32)) * scale
        dist = (base_b + jnp.arange(2, dtype=jnp.int32)[:, None] - jnp.arange(BLK, dtype=jnp.int32)[None, :]).astype(jnp.float32)
        scores = scores - slopes[None, :, None] * dist[:, None, :]
        top = lax.optimization_barrier(jnp.max(scores, axis=-1))
        probs = jnp.exp(scores - top[..., None])
        total = lax.optimization_barrier(jnp.sum(probs, axis=-1))
        weights = probs.astype(jnp.bfloat16)
        acc = jnp.einsum('sht,thd->shd', weights.astype(jnp.float32), values_b.astype(jnp.float32))
        top = jnp.where(live_b, top, NEG)
        total = jnp.where(live_b, total, 0.0)
        acc = jnp.where(live_b, acc, 0.0)
        return (top, total, acc)
    tops, totals, accs = lax.map(block_term, (keys, values, block_query, base, live))
    rowhot = (block_row[:, None] == jnp.arange(REQ, dtype=jnp.int32)[None, :]) & live[:, None]
    tab_top = lax.optimization_barrier(jnp.max(jnp.where(rowhot[:, :, None, None], tops[:, None], NEG), axis=0))
    ratio = jnp.exp(tops - jnp.take(tab_top, block_row, axis=0))
    tab_sum = jax.ops.segment_sum(ratio * totals, block_row, num_segments=REQ)
    tab_acc = jax.ops.segment_sum(ratio[..., None] * accs, block_row, num_segments=REQ)
    tab_top = tab_top.transpose(1, 0, 2)
    tab_sum = tab_sum.transpose(1, 0, 2)
    tab_acc = tab_acc.transpose(1, 0, 2, 3)
    own_top, own_sum, own_acc = self_terms(queries.reshape(2, REQ, HEADS, HDIM), new_keys.reshape(2, REQ, HEADS, HDIM), new_values.reshape(2, REQ, HEADS, HDIM), slopes, scale)
    top = jnp.maximum(tab_top, own_top)
    wa = jnp.exp(tab_top - top)
    wb = jnp.exp(own_top - top)
    total = tab_sum * wa + own_sum * wb
    acc = tab_acc * wa[..., None] + own_acc * wb[..., None]
    attended = (acc / total[..., None]).astype(jnp.bfloat16).reshape(2 * REQ, HEADS * HDIM)
    projected = jnp.dot(attended, out_weight, preferred_element_type=jnp.float32).reshape(2, REQ, D)
    return (residual.astype(jnp.float32) + projected).astype(jnp.bfloat16)
```

```python
import functools
import math

import jax
import jax.numpy as jnp
from jax import lax
from jax.experimental import pallas as pl
from jax.experimental.pallas import tpu as pltpu
from jax.sharding import PartitionSpec as P

BLK = 128
FAR = 1e35
MESH = pl.DeviceIdType.MESH


def kernel(
    n_seq,
    n_head,
    heads,
    unit,
    tile,
    own_ref,
    seg_ref,
    row_ref,
    slope_ref,
    res_ref,
    k_hbm,
    v_hbm,
    w_hbm,
    out_ref,
    kbuf,
    vbuf,
    wbuf,
    qall,
    q2d,
    dist,
    o2d,
    st2d,
    sendb,
    recvb,
    attb,
    x_ref,
    shares,
    got,
    k_sem,
    v_sem,
    w_sem,
    q_send,
    q_recv,
    p_send,
    p_recv,
    a_send,
    a_recv,
    h_send,
    h_recv,
):
    hdim = own_ref.shape[3]
    rows = 2 * n_seq
    per = n_seq // n_head
    tokens = k_hbm.shape[0]
    padded = q2d.shape[0] // rows
    groups = heads // unit
    wide = unit * hdim
    cols = w_hbm.shape[1]
    scale = 1.0 / math.sqrt(hdim)
    me = lax.axis_index("seq")
    mine = lax.axis_index("head")

    def k_copy(g):
        at = pl.ds(pl.multiple_of(g * wide, 128), wide)
        return pltpu.make_async_copy(k_hbm.at[:, at], kbuf.at[:, at], k_sem.at[g])

    def v_copy(g):
        at = pl.ds(pl.multiple_of(g * wide, 128), wide)
        return pltpu.make_async_copy(v_hbm.at[:, at], vbuf.at[:, at], v_sem.at[g])

    def w_copy(g):
        at = pl.ds(pl.multiple_of(g * wide, 128), wide)
        return pltpu.make_async_copy(w_hbm.at[at], wbuf.at[at], w_sem.at[g])

    def to_seq(step):
        return lax.rem(me + step, n_seq)

    def to_head(step):
        return lax.rem(mine + step, n_head)

    barrier = pltpu.get_barrier_semaphore()
    for step in range(1, n_seq):
        pl.semaphore_signal(
            barrier, inc=1, device_id={"seq": to_seq(step)}, device_id_type=MESH
        )
    for step in range(1, n_head):
        pl.semaphore_signal(
            barrier, inc=1, device_id={"head": to_head(step)}, device_id_type=MESH
        )
    for g in range(groups):
        k_copy(g).start()
        v_copy(g).start()
    for g in range(groups):
        w_copy(g).start()
    pl.semaphore_wait(barrier, n_seq + n_head - 2)

    def q_copy(step):
        return pltpu.make_async_remote_copy(
            src_ref=own_ref.at[0],
            dst_ref=qall.at[me],
            send_sem=q_send.at[step - 1],
            recv_sem=q_recv.at[step - 1],
            device_id={"seq": to_seq(step)},
            device_id_type=MESH,
        )

    for step in range(1, n_seq):
        q_copy(step).start()

    line = lax.broadcasted_iota(jnp.int32, (rows, 1), 0)
    begin = jnp.zeros((rows, 1), jnp.int32)
    end = jnp.zeros((rows, 1), jnp.int32)
    at = jnp.int32(0)
    for i in range(n_seq):
        after = at + seg_ref[i]
        hit = (line // 2) == row_ref[i]
        begin = jnp.where(hit, at * BLK, begin)
        end = jnp.where(hit, after * BLK, end)
        at = after
    token = me * tokens + lax.broadcasted_iota(jnp.int32, (rows, tokens), 1)
    gap = (end + lax.rem(line, 2) - token).astype(jnp.float32)
    dist[...] = jnp.where((token >= begin) & (token < end), gap, FAR)

    lane = lax.broadcasted_iota(jnp.int32, (heads, hdim), 1)
    own = own_ref[...].astype(jnp.float32)
    slope_col = jnp.zeros((heads, 1), jnp.float32)
    hline = lax.broadcasted_iota(jnp.int32, (heads, 1), 0)
    for h in range(heads):
        slope_col = jnp.where(hline == h, slope_ref[h], slope_col)
    e00 = jnp.sum(own[0, 0] * own[1, 0], axis=-1, keepdims=True) * scale
    e10 = jnp.sum(own[0, 1] * own[1, 0], axis=-1, keepdims=True) * scale - slope_col
    e11 = jnp.sum(own[0, 1] * own[1, 1], axis=-1, keepdims=True) * scale
    upper = jnp.maximum(e10, e11)
    w10 = jnp.exp(e10 - upper)
    w11 = jnp.exp(e11 - upper)
    own_stat = jnp.where(
        lane == 0,
        e00,
        jnp.where(lane == 1, 1.0, jnp.where(lane == 2, upper, w10 + w11)),
    )
    own_acc = [own[2, 0], w10 * own[2, 0] + w11 * own[2, 1]]

    qall[me] = own_ref[0]
    for step in range(1, n_seq):
        q_copy(step).wait_recv()
    for r in range(n_seq):
        for s in range(2):
            q2d[pl.ds((2 * r + s) * padded, heads), :] = qall[r, s].astype(jnp.float32)

    odd = lax.rem(lax.broadcasted_iota(jnp.int32, (rows, hdim), 1), 2) == 1

    def attend(g, _):
        k_copy(g).wait()
        v_copy(g).wait()
        for u in range(unit):
            h = g * unit + u
            at = pl.ds(pl.multiple_of(h * hdim, 128), hdim)
            query = q2d[pl.ds(h, rows, stride=padded), :].astype(jnp.bfloat16)
            score = (
                lax.dot_general(
                    query,
                    kbuf[:, at],
                    (((1,), (1,)), ((), ())),
                    preferred_element_type=jnp.float32,
                )
                * scale
                - slope_ref[h] * dist[...]
            )
            top = jnp.max(score, axis=-1, keepdims=True)
            prob = jnp.exp(score - top)
            total = jnp.sum(prob, axis=-1, keepdims=True)
            put = pl.ds(pl.multiple_of(h * rows, 8), rows)
            o2d[put, :] = jnp.dot(
                prob.astype(jnp.bfloat16), vbuf[:, at], preferred_element_type=jnp.float32
            )
            st2d[put, :] = jnp.where(odd, total, top)
        return 0

    lax.fori_loop(0, groups, attend, 0)

    for r in range(n_seq):
        first = st2d[pl.ds(2 * r, heads, stride=rows), :]
        second = st2d[pl.ds(2 * r + 1, heads, stride=rows), :]
        stat = jnp.where(lax.rem(lane, 4) < 2, first, second)
        high = stat.astype(jnp.bfloat16).astype(jnp.float32)
        rest = stat - high
        middle = rest.astype(jnp.bfloat16).astype(jnp.float32)
        low = rest - middle
        sendb[r, 2] = jnp.where(lane < 4, high, jnp.where(lane < 8, middle, low)).astype(
            jnp.bfloat16
        )
        for s in range(2):
            sendb[r, s] = o2d[pl.ds(2 * r + s, heads, stride=rows), :].astype(jnp.bfloat16)

    def p_copy(step):
        return pltpu.make_async_remote_copy(
            src_ref=sendb.at[to_seq(step)],
            dst_ref=recvb.at[me],
            send_sem=p_send.at[step - 1],
            recv_sem=p_recv.at[step - 1],
            device_id={"seq": to_seq(step)},
            device_id_type=MESH,
        )

    for step in range(1, n_seq):
        p_copy(step).start()
    recvb[me] = sendb[me]
    for step in range(1, n_seq):
        p_copy(step).wait_recv()

    stats = [own_stat]
    for j in range(n_seq):
        x = recvb[j, 2].astype(jnp.float32)
        x = x + pltpu.roll(x, hdim - 4, 1) + pltpu.roll(x, hdim - 8, 1)
        stats.append(x)
    highest = functools.reduce(jnp.maximum, stats)
    factors = [jnp.exp(jnp.minimum(x - highest, 0.0)) for x in stats]
    total = sum(f * pltpu.roll(x, hdim - 1, 1) for f, x in zip(factors, stats))
    inverse = 1.0 / total
    pair = lax.div(me, per)
    place = lax.rem(me, per)
    for s in range(2):
        inv = inverse[:, 2 * s : 2 * s + 1]
        acc = factors[0][:, 2 * s : 2 * s + 1] * own_acc[s]
        for j in range(n_seq):
            acc += factors[j + 1][:, 2 * s : 2 * s + 1] * recvb[j, s].astype(jnp.float32)
        attb[pair, place, s] = (acc * inv).astype(jnp.bfloat16)

    def a_copy(step):
        return pltpu.make_async_remote_copy(
            src_ref=attb.at[pair, place],
            dst_ref=attb.at[pair, place],
            send_sem=a_send.at[step - 1],
            recv_sem=a_recv.at[step - 1],
            device_id={"seq": to_seq(step)},
            device_id_type=MESH,
        )

    def a_wait(step):
        source = lax.rem(me + n_seq - step, n_seq)
        here = attb.at[lax.div(source, per), lax.rem(source, per)]
        return pltpu.make_async_remote_copy(
            src_ref=here,
            dst_ref=here,
            send_sem=a_send.at[step - 1],
            recv_sem=a_recv.at[step - 1],
            device_id={"seq": to_seq(step)},
            device_id_type=MESH,
        )

    for step in range(1, n_seq):
        a_copy(step).start()
    for g in range(groups):
        w_copy(g).wait()
    for step in range(1, n_seq):
        a_wait(step).wait_recv()
    for k in range(n_head):
        for s in range(2):
            for j in range(per):
                n = (k * 2 + s) * per + j
                q2d[pl.ds(n * padded, heads), :] = attb[k, j, s].astype(jnp.float32)
    for h in range(heads):
        x_ref[:, h * hdim : (h + 1) * hdim] = q2d[pl.ds(h, rows, stride=padded), :].astype(
            jnp.bfloat16
        )

    for c in range(cols // tile):
        at = slice(c * tile, (c + 1) * tile)
        part = jnp.dot(x_ref[...], wbuf[:, at], preferred_element_type=jnp.float32)
        for k in range(n_head):
            shares[k, :, at] = part[2 * per * k : 2 * per * (k + 1)].astype(jnp.bfloat16)

    def h_copy(step):
        return pltpu.make_async_remote_copy(
            src_ref=shares.at[to_head(step)],
            dst_ref=got.at[step - 1],
            send_sem=h_send.at[step - 1],
            recv_sem=h_recv.at[step - 1],
            device_id={"head": to_head(step)},
            device_id_type=MESH,
        )

    for step in range(1, n_head):
        h_copy(step).start()
    summed = shares[mine].astype(jnp.float32)
    for step in range(1, n_head):
        h_copy(step).wait_recv()
        summed += got[step - 1].astype(jnp.float32)
    for s in range(2):
        out_ref[s] = (
            res_ref[s].astype(jnp.float32) + summed[s * per : (s + 1) * per]
        ).astype(jnp.bfloat16)
    for step in range(1, n_seq):
        q_copy(step).wait_send()
        p_copy(step).wait_send()
        a_copy(step).wait_send()
    for step in range(1, n_head):
        h_copy(step).wait_send()


def body(
    n_seq,
    n_head,
    queries,
    new_keys,
    new_values,
    cache_keys,
    cache_values,
    slopes,
    seg_blocks,
    request_row,
    out_weight,
    residual,
):
    heads = slopes.shape[0]
    width = queries.shape[2]
    hdim = width // heads
    tokens = cache_keys.shape[0]
    cols = out_weight.shape[1]
    assert queries.shape[1] == 1 and seg_blocks.shape[0] == n_seq
    own = jnp.stack([queries, new_keys, new_values]).reshape(3, 2, heads, hdim)
    unit = max(u for u in (1, 2, 4) if heads % u == 0)
    tile = 256 if cols % 256 == 0 else cols
    rows = 2 * n_seq
    per = n_seq // n_head
    padded = -(-heads // 8) * 8
    groups = heads // unit
    bf16, f32 = jnp.bfloat16, jnp.float32
    dma = pltpu.SemaphoreType.DMA
    vmem = pl.BlockSpec(memory_space=pltpu.VMEM)
    smem = pl.BlockSpec(memory_space=pltpu.SMEM)
    hbm = pl.BlockSpec(memory_space=pl.ANY)
    return pl.pallas_call(
        functools.partial(kernel, n_seq, n_head, heads, unit, tile),
        out_shape=jax.ShapeDtypeStruct(residual.shape, residual.dtype),
        in_specs=[vmem, smem, smem, smem, vmem, hbm, hbm, hbm],
        out_specs=vmem,
        scratch_shapes=[
            pltpu.VMEM(cache_keys.shape, bf16),
            pltpu.VMEM(cache_values.shape, bf16),
            pltpu.VMEM(out_weight.shape, bf16),
            pltpu.VMEM((n_seq, 2, heads, hdim), bf16),
            pltpu.VMEM((rows * padded, hdim), f32),
            pltpu.VMEM((rows, tokens), f32),
            pltpu.VMEM((heads * rows, hdim), f32),
            pltpu.VMEM((heads * rows, hdim), f32),
            pltpu.VMEM((n_seq, 3, heads, hdim), bf16),
            pltpu.VMEM((n_seq, 3, heads, hdim), bf16),
            pltpu.VMEM((n_head, per, 2, heads, hdim), bf16),
            pltpu.VMEM((rows, width), bf16),
            pltpu.VMEM((n_head, 2 * per, cols), bf16),
            pltpu.VMEM((n_head - 1, 2 * per, cols), bf16),
            dma((groups,)),
            dma((groups,)),
            dma((groups,)),
            dma((n_seq - 1,)),
            dma((n_seq - 1,)),
            dma((n_seq - 1,)),
            dma((n_seq - 1,)),
            dma((n_seq - 1,)),
            dma((n_seq - 1,)),
            dma((n_head - 1,)),
            dma((n_head - 1,)),
        ],
        compiler_params=pltpu.CompilerParams(
            collective_id=0, has_side_effects=True, vmem_limit_bytes=56 << 20
        ),
    )(own, seg_blocks, request_row, slopes, residual, cache_keys, cache_values, out_weight)


def solution(mesh):
    in_specs = (
        P(None, "seq", "head"),
        P(None, "seq", "head"),
        P(None, "seq", "head"),
        P("seq", "head"),
        P("seq", "head"),
        P("head"),
        P(),
        P(),
        P("head", "seq"),
        P(None, "head", "seq"),
    )
    out_specs = P(None, "head", "seq")
    sizes = (mesh.shape["seq"], mesh.shape["head"])
    return jax.shard_map(
        functools.partial(body, *sizes),
        mesh=mesh,
        in_specs=in_specs,
        out_specs=out_specs,
        check_vma=False,
    )
```

```python
import functools
import math

import jax
import jax.numpy as jnp
from jax import lax
from jax.experimental import pallas as pl
from jax.experimental.pallas import tpu as pltpu
from jax.sharding import PartitionSpec as P

BLK = 128
FAR = 1e35
LAG = 3
MESH = pl.DeviceIdType.MESH


def kernel(
    n_seq,
    n_head,
    heads,
    unit,
    tile,
    qry_ref,
    key_ref,
    val_ref,
    seg_ref,
    row_ref,
    slope_ref,
    res_ref,
    k_hbm,
    v_hbm,
    w_hbm,
    out_ref,
    kbuf,
    vbuf,
    wbuf,
    qall,
    own2d,
    qx,
    sbuf,
    pbuf,
    q2d,
    dist,
    o2d,
    st2d,
    sendb,
    recvb,
    attb,
    x_ref,
    shares,
    got,
    k_sem,
    v_sem,
    w_sem,
    q_send,
    q_recv,
    p_send,
    p_recv,
    a_send,
    a_recv,
    h_send,
    h_recv,
):
    hdim = qry_ref.shape[1] // heads
    rows = 2 * n_seq
    per = n_seq // n_head
    tokens = k_hbm.shape[0]
    padded = q2d.shape[0] // rows
    groups = heads // unit
    wide = unit * hdim
    cols = w_hbm.shape[1]
    scale = 1.0 / math.sqrt(hdim)
    me = lax.axis_index("seq")
    mine = lax.axis_index("head")

    def k_copy(g):
        at = pl.ds(pl.multiple_of(g * wide, 128), wide)
        return pltpu.make_async_copy(k_hbm.at[:, at], kbuf.at[:, at], k_sem.at[g])

    def v_copy(g):
        at = pl.ds(pl.multiple_of(g * wide, 128), wide)
        return pltpu.make_async_copy(v_hbm.at[:, at], vbuf.at[:, at], v_sem.at[g])

    def w_copy(g):
        at = pl.ds(pl.multiple_of(g * wide, 128), wide)
        return pltpu.make_async_copy(w_hbm.at[at], wbuf.at[at], w_sem.at[g])

    def to_seq(step):
        return lax.rem(me + step, n_seq)

    def to_head(step):
        return lax.rem(mine + step, n_head)

    barrier = pltpu.get_barrier_semaphore()
    for step in range(1, n_seq):
        pl.semaphore_signal(
            barrier, inc=1, device_id={"seq": to_seq(step)}, device_id_type=MESH
        )
    for step in range(1, n_head):
        pl.semaphore_signal(
            barrier, inc=1, device_id={"head": to_head(step)}, device_id_type=MESH
        )
    for g in range(groups):
        k_copy(g).start()
        v_copy(g).start()
    for g in range(groups):
        w_copy(g).start()
    pl.semaphore_wait(barrier, n_seq + n_head - 2)

    def q_copy(step):
        return pltpu.make_async_remote_copy(
            src_ref=qry_ref,
            dst_ref=qall.at[me],
            send_sem=q_send.at[step - 1],
            recv_sem=q_recv.at[step - 1],
            device_id={"seq": to_seq(step)},
            device_id_type=MESH,
        )

    for step in range(1, n_seq):
        q_copy(step).start()

    line = lax.broadcasted_iota(jnp.int32, (rows, 1), 0)
    begin = jnp.zeros((rows, 1), jnp.int32)
    end = jnp.zeros((rows, 1), jnp.int32)
    at = jnp.int32(0)
    for i in range(n_seq):
        after = at + seg_ref[i]
        hit = (line // 2) == row_ref[i]
        begin = jnp.where(hit, at * BLK, begin)
        end = jnp.where(hit, after * BLK, end)
        at = after
    token = me * tokens + lax.broadcasted_iota(jnp.int32, (rows, tokens), 1)
    gap = (end + lax.rem(line, 2) - token).astype(jnp.float32)
    dist[...] = jnp.where((token >= begin) & (token < end), gap, FAR)

    lane = lax.broadcasted_iota(jnp.int32, (heads, hdim), 1)
    for n, ref in enumerate((qry_ref, key_ref, val_ref)):
        for h in range(heads):
            own2d[n, 2 * h : 2 * h + 2, :] = ref[:, h * hdim : (h + 1) * hdim].astype(jnp.float32)
    own = [
        [own2d.at[n][pl.ds(t, heads, stride=2), :] for t in range(2)] for n in range(3)
    ]
    slope_col = jnp.zeros((heads, 1), jnp.float32)
    hline = lax.broadcasted_iota(jnp.int32, (heads, 1), 0)
    for h in range(heads):
        slope_col = jnp.where(hline == h, slope_ref[h], slope_col)
    e00 = jnp.sum(own[0][0] * own[1][0], axis=-1, keepdims=True) * scale
    e10 = jnp.sum(own[0][1] * own[1][0], axis=-1, keepdims=True) * scale - slope_col
    e11 = jnp.sum(own[0][1] * own[1][1], axis=-1, keepdims=True) * scale
    upper = jnp.maximum(e10, e11)
    w10 = jnp.exp(e10 - upper)
    w11 = jnp.exp(e11 - upper)
    own_stat = jnp.where(
        lane == 0,
        e00,
        jnp.where(lane == 1, 1.0, jnp.where(lane == 2, upper, w10 + w11)),
    )
    own_acc = [own[2][0], w10 * own[2][0] + w11 * own[2][1]]

    qall[me] = qry_ref[...]
    for step in range(1, n_seq):
        q_copy(step).wait_recv()
    for r in range(n_seq):
        qx[2 * r : 2 * r + 2, :] = qall[r].astype(jnp.float32)

    odd = lax.rem(lax.broadcasted_iota(jnp.int32, (rows, hdim), 1), 2) == 1

    def lanes(h):
        return slice(h * hdim, (h + 1) * hdim)

    def lines(h):
        return slice(h * rows, (h + 1) * rows)

    def scores(h):
        if h % unit == 0:
            k_copy(h // unit).wait()
        dots = lax.dot_general(
            qx[:, lanes(h)].astype(jnp.bfloat16),
            kbuf[:, lanes(h)],
            (((1,), (1,)), ((), ())),
            preferred_element_type=jnp.float32,
        )
        sbuf[lines(h), :] = dots * scale - slope_ref[h] * dist[...]

    def soften(h):
        score = sbuf[lines(h), :]
        top = jnp.max(score, axis=-1, keepdims=True)
        prob = jnp.exp(score - top)
        total = jnp.sum(prob, axis=-1, keepdims=True)
        pbuf[lines(h), :] = prob.astype(jnp.bfloat16)
        st2d[lines(h), :] = jnp.where(odd, total, top)

    def weigh(h):
        if h % unit == 0:
            v_copy(h // unit).wait()
        o2d[lines(h), :] = jnp.dot(
            pbuf[lines(h), :], vbuf[:, lanes(h)], preferred_element_type=jnp.float32
        )

    for h in range(heads + 2 * LAG):
        if h < heads:
            scores(h)
        if 0 <= h - LAG < heads:
            soften(h - LAG)
        if 0 <= h - 2 * LAG:
            weigh(h - 2 * LAG)

    for r in range(n_seq):
        first = st2d[pl.ds(2 * r, heads, stride=rows), :]
        second = st2d[pl.ds(2 * r + 1, heads, stride=rows), :]
        stat = jnp.where(lax.rem(lane, 4) < 2, first, second)
        high = stat.astype(jnp.bfloat16).astype(jnp.float32)
        rest = stat - high
        middle = rest.astype(jnp.bfloat16).astype(jnp.float32)
        low = rest - middle
        sendb[r, 2] = jnp.where(lane < 4, high, jnp.where(lane < 8, middle, low)).astype(
            jnp.bfloat16
        )
        for s in range(2):
            sendb[r, s] = o2d[pl.ds(2 * r + s, heads, stride=rows), :].astype(jnp.bfloat16)

    def p_copy(step):
        return pltpu.make_async_remote_copy(
            src_ref=sendb.at[to_seq(step)],
            dst_ref=recvb.at[me],
            send_sem=p_send.at[step - 1],
            recv_sem=p_recv.at[step - 1],
            device_id={"seq": to_seq(step)},
            device_id_type=MESH,
        )

    for step in range(1, n_seq):
        p_copy(step).start()
    recvb[me] = sendb[me]
    for step in range(1, n_seq):
        p_copy(step).wait_recv()

    stats = [own_stat]
    for j in range(n_seq):
        x = recvb[j, 2].astype(jnp.float32)
        x = x + pltpu.roll(x, hdim - 4, 1) + pltpu.roll(x, hdim - 8, 1)
        stats.append(x)
    highest = functools.reduce(jnp.maximum, stats)
    factors = [jnp.exp(jnp.minimum(x - highest, 0.0)) for x in stats]
    total = sum(f * pltpu.roll(x, hdim - 1, 1) for f, x in zip(factors, stats))
    inverse = 1.0 / total
    pair = lax.div(me, per)
    place = lax.rem(me, per)
    for s in range(2):
        inv = inverse[:, 2 * s : 2 * s + 1]
        acc = factors[0][:, 2 * s : 2 * s + 1] * own_acc[s]
        for j in range(n_seq):
            acc += factors[j + 1][:, 2 * s : 2 * s + 1] * recvb[j, s].astype(jnp.float32)
        attb[pair, place, s] = (acc * inv).astype(jnp.bfloat16)

    def a_copy(step):
        return pltpu.make_async_remote_copy(
            src_ref=attb.at[pair, place],
            dst_ref=attb.at[pair, place],
            send_sem=a_send.at[step - 1],
            recv_sem=a_recv.at[step - 1],
            device_id={"seq": to_seq(step)},
            device_id_type=MESH,
        )

    def a_wait(step):
        source = lax.rem(me + n_seq - step, n_seq)
        here = attb.at[lax.div(source, per), lax.rem(source, per)]
        return pltpu.make_async_remote_copy(
            src_ref=here,
            dst_ref=here,
            send_sem=a_send.at[step - 1],
            recv_sem=a_recv.at[step - 1],
            device_id={"seq": to_seq(step)},
            device_id_type=MESH,
        )

    for step in range(1, n_seq):
        a_copy(step).start()
    for g in range(groups):
        w_copy(g).wait()
    for step in range(1, n_seq):
        a_wait(step).wait_recv()
    for k in range(n_head):
        for s in range(2):
            for j in range(per):
                n = (k * 2 + s) * per + j
                q2d[pl.ds(n * padded, heads), :] = attb[k, j, s].astype(jnp.float32)
    for h in range(heads):
        x_ref[:, h * hdim : (h + 1) * hdim] = q2d[pl.ds(h, rows, stride=padded), :].astype(
            jnp.bfloat16
        )

    for c in range(cols // tile):
        at = slice(c * tile, (c + 1) * tile)
        part = jnp.dot(x_ref[...], wbuf[:, at], preferred_element_type=jnp.float32)
        for k in range(n_head):
            shares[k, :, at] = part[2 * per * k : 2 * per * (k + 1)].astype(jnp.bfloat16)

    def h_copy(step):
        return pltpu.make_async_remote_copy(
            src_ref=shares.at[to_head(step)],
            dst_ref=got.at[step - 1],
            send_sem=h_send.at[step - 1],
            recv_sem=h_recv.at[step - 1],
            device_id={"head": to_head(step)},
            device_id_type=MESH,
        )

    for step in range(1, n_head):
        h_copy(step).start()
    summed = shares[mine].astype(jnp.float32)
    for step in range(1, n_head):
        h_copy(step).wait_recv()
        summed += got[step - 1].astype(jnp.float32)
    for s in range(2):
        out_ref[s] = (
            res_ref[s].astype(jnp.float32) + summed[s * per : (s + 1) * per]
        ).astype(jnp.bfloat16)
    for step in range(1, n_seq):
        q_copy(step).wait_send()
        p_copy(step).wait_send()
        a_copy(step).wait_send()
    for step in range(1, n_head):
        h_copy(step).wait_send()


def body(
    n_seq,
    n_head,
    queries,
    new_keys,
    new_values,
    cache_keys,
    cache_values,
    slopes,
    seg_blocks,
    request_row,
    out_weight,
    residual,
):
    heads = slopes.shape[0]
    width = queries.shape[2]
    hdim = width // heads
    tokens = cache_keys.shape[0]
    cols = out_weight.shape[1]
    assert queries.shape[1] == 1 and seg_blocks.shape[0] == n_seq
    flat = [x.reshape(2, width) for x in (queries, new_keys, new_values)]
    unit = max(u for u in (1, 2, 4) if heads % u == 0)
    tile = 256 if cols % 256 == 0 else cols
    rows = 2 * n_seq
    per = n_seq // n_head
    padded = -(-heads // 8) * 8
    groups = heads // unit
    bf16, f32 = jnp.bfloat16, jnp.float32
    dma = pltpu.SemaphoreType.DMA
    vmem = pl.BlockSpec(memory_space=pltpu.VMEM)
    smem = pl.BlockSpec(memory_space=pltpu.SMEM)
    hbm = pl.BlockSpec(memory_space=pl.ANY)
    return pl.pallas_call(
        functools.partial(kernel, n_seq, n_head, heads, unit, tile),
        out_shape=jax.ShapeDtypeStruct(residual.shape, residual.dtype),
        in_specs=[vmem, vmem, vmem, smem, smem, smem, vmem, hbm, hbm, hbm],
        out_specs=vmem,
        scratch_shapes=[
            pltpu.VMEM(cache_keys.shape, bf16),
            pltpu.VMEM(cache_values.shape, bf16),
            pltpu.VMEM(out_weight.shape, bf16),
            pltpu.VMEM((n_seq, 2, width), bf16),
            pltpu.VMEM((3, 2 * heads, hdim), f32),
            pltpu.VMEM((rows, width), f32),
            pltpu.VMEM((heads * rows, tokens), f32),
            pltpu.VMEM((heads * rows, tokens), bf16),
            pltpu.VMEM((rows * padded, hdim), f32),
            pltpu.VMEM((rows, tokens), f32),
            pltpu.VMEM((heads * rows, hdim), f32),
            pltpu.VMEM((heads * rows, hdim), f32),
            pltpu.VMEM((n_seq, 3, heads, hdim), bf16),
            pltpu.VMEM((n_seq, 3, heads, hdim), bf16),
            pltpu.VMEM((n_head, per, 2, heads, hdim), bf16),
            pltpu.VMEM((rows, width), bf16),
            pltpu.VMEM((n_head, 2 * per, cols), bf16),
            pltpu.VMEM((n_head - 1, 2 * per, cols), bf16),
            dma((groups,)),
            dma((groups,)),
            dma((groups,)),
            dma((n_seq - 1,)),
            dma((n_seq - 1,)),
            dma((n_seq - 1,)),
            dma((n_seq - 1,)),
            dma((n_seq - 1,)),
            dma((n_seq - 1,)),
            dma((n_head - 1,)),
            dma((n_head - 1,)),
        ],
        compiler_params=pltpu.CompilerParams(
            collective_id=0, has_side_effects=True, vmem_limit_bytes=56 << 20
        ),
    )(*flat, seg_blocks, request_row, slopes, residual, cache_keys, cache_values, out_weight)


def solution(mesh):
    in_specs = (
        P(None, "seq", "head"),
        P(None, "seq", "head"),
        P(None, "seq", "head"),
        P("seq", "head"),
        P("seq", "head"),
        P("head"),
        P(),
        P(),
        P("head", "seq"),
        P(None, "head", "seq"),
    )
    out_specs = P(None, "head", "seq")
    sizes = (mesh.shape["seq"], mesh.shape["head"])
    return jax.shard_map(
        functools.partial(body, *sizes),
        mesh=mesh,
        in_specs=in_specs,
        out_specs=out_specs,
        check_vma=False,
    )
```

```python
import functools
import math

import jax
import jax.numpy as jnp
from jax import lax
from jax.experimental import pallas as pl
from jax.experimental.pallas import tpu as pltpu
from jax.sharding import PartitionSpec as P

BLK = 128
FAR = 1e35
LAG = 3
PARTS = 2
MESH = pl.DeviceIdType.MESH


def kernel(
    n_seq,
    n_head,
    heads,
    unit,
    tile,
    qry_ref,
    key_ref,
    val_ref,
    seg_ref,
    row_ref,
    slope_ref,
    res_ref,
    k_hbm,
    v_hbm,
    w_hbm,
    out_ref,
    kbuf,
    vbuf,
    wbuf,
    qall,
    own2d,
    qx,
    sbuf,
    pbuf,
    q2d,
    dist,
    o2d,
    st2d,
    sendb,
    recvb,
    attb,
    x_ref,
    sofar,
    shares,
    got,
    k_sem,
    v_sem,
    w_sem,
    q_send,
    q_recv,
    p_send,
    p_recv,
    a_send,
    a_recv,
    h_send,
    h_recv,
):
    hdim = qry_ref.shape[1] // heads
    rows = 2 * n_seq
    per = n_seq // n_head
    tokens = k_hbm.shape[0]
    padded = q2d.shape[0] // rows
    groups = heads // unit
    some = heads // PARTS
    slot = padded // PARTS
    wide = unit * hdim
    cols = w_hbm.shape[1]
    scale = 1.0 / math.sqrt(hdim)
    me = lax.axis_index("seq")
    mine = lax.axis_index("head")

    def k_copy(g):
        at = pl.ds(pl.multiple_of(g * wide, 128), wide)
        return pltpu.make_async_copy(k_hbm.at[:, at], kbuf.at[:, at], k_sem.at[g])

    def v_copy(g):
        at = pl.ds(pl.multiple_of(g * wide, 128), wide)
        return pltpu.make_async_copy(v_hbm.at[:, at], vbuf.at[:, at], v_sem.at[g])

    def w_copy(g):
        at = pl.ds(pl.multiple_of(g * wide, 128), wide)
        return pltpu.make_async_copy(w_hbm.at[at], wbuf.at[at], w_sem.at[g])

    def to_seq(step):
        return lax.rem(me + step, n_seq)

    def to_head(step):
        return lax.rem(mine + step, n_head)

    barrier = pltpu.get_barrier_semaphore()
    for step in range(1, n_seq):
        pl.semaphore_signal(
            barrier, inc=1, device_id={"seq": to_seq(step)}, device_id_type=MESH
        )
    for step in range(1, n_head):
        pl.semaphore_signal(
            barrier, inc=1, device_id={"head": to_head(step)}, device_id_type=MESH
        )
    for g in range(groups):
        k_copy(g).start()
        v_copy(g).start()
    for g in range(groups):
        w_copy(g).start()
    pl.semaphore_wait(barrier, n_seq + n_head - 2)

    def q_copy(step):
        return pltpu.make_async_remote_copy(
            src_ref=qry_ref,
            dst_ref=qall.at[me],
            send_sem=q_send.at[step - 1],
            recv_sem=q_recv.at[step - 1],
            device_id={"seq": to_seq(step)},
            device_id_type=MESH,
        )

    for step in range(1, n_seq):
        q_copy(step).start()

    line = lax.broadcasted_iota(jnp.int32, (rows, 1), 0)
    begin = jnp.zeros((rows, 1), jnp.int32)
    end = jnp.zeros((rows, 1), jnp.int32)
    at = jnp.int32(0)
    for i in range(n_seq):
        after = at + seg_ref[i]
        hit = (line // 2) == row_ref[i]
        begin = jnp.where(hit, at * BLK, begin)
        end = jnp.where(hit, after * BLK, end)
        at = after
    token = me * tokens + lax.broadcasted_iota(jnp.int32, (rows, tokens), 1)
    gap = (end + lax.rem(line, 2) - token).astype(jnp.float32)
    dist[...] = jnp.where((token >= begin) & (token < end), gap, FAR)

    lane = lax.broadcasted_iota(jnp.int32, (some, hdim), 1)
    hline = lax.broadcasted_iota(jnp.int32, (some, 1), 0)
    for n, ref in enumerate((qry_ref, key_ref, val_ref)):
        for h in range(heads):
            own2d[n, 2 * h : 2 * h + 2, :] = ref[:, h * hdim : (h + 1) * hdim].astype(jnp.float32)

    def own_terms(p):
        own = [
            [own2d.at[n][pl.ds(2 * p * some + t, some, stride=2), :] for t in range(2)]
            for n in range(3)
        ]
        slope_col = jnp.zeros((some, 1), jnp.float32)
        for h in range(some):
            slope_col = jnp.where(hline == h, slope_ref[p * some + h], slope_col)
        e00 = jnp.sum(own[0][0] * own[1][0], axis=-1, keepdims=True) * scale
        e10 = jnp.sum(own[0][1] * own[1][0], axis=-1, keepdims=True) * scale - slope_col
        e11 = jnp.sum(own[0][1] * own[1][1], axis=-1, keepdims=True) * scale
        upper = jnp.maximum(e10, e11)
        w10 = jnp.exp(e10 - upper)
        w11 = jnp.exp(e11 - upper)
        stat = jnp.where(
            lane == 0,
            e00,
            jnp.where(lane == 1, 1.0, jnp.where(lane == 2, upper, w10 + w11)),
        )
        return stat, [own[2][0], w10 * own[2][0] + w11 * own[2][1]]

    owned = [own_terms(p) for p in range(PARTS)]

    qall[me] = qry_ref[...]
    for step in range(1, n_seq):
        q_copy(step).wait_recv()
    for r in range(n_seq):
        qx[2 * r : 2 * r + 2, :] = qall[r].astype(jnp.float32)

    odd = lax.rem(lax.broadcasted_iota(jnp.int32, (rows, hdim), 1), 2) == 1

    def lanes(h):
        return slice(h * hdim, (h + 1) * hdim)

    def lines(h):
        return slice(h * rows, (h + 1) * rows)

    def scores(h):
        if h % unit == 0:
            k_copy(h // unit).wait()
        dots = lax.dot_general(
            qx[:, lanes(h)].astype(jnp.bfloat16),
            kbuf[:, lanes(h)],
            (((1,), (1,)), ((), ())),
            preferred_element_type=jnp.float32,
        )
        sbuf[lines(h), :] = dots * scale - slope_ref[h] * dist[...]

    def soften(h):
        score = sbuf[lines(h), :]
        top = jnp.max(score, axis=-1, keepdims=True)
        prob = jnp.exp(score - top)
        total = jnp.sum(prob, axis=-1, keepdims=True)
        pbuf[lines(h), :] = prob.astype(jnp.bfloat16)
        st2d[lines(h), :] = jnp.where(odd, total, top)

    def weigh(h):
        if h % unit == 0:
            v_copy(h // unit).wait()
        o2d[lines(h), :] = jnp.dot(
            pbuf[lines(h), :], vbuf[:, lanes(h)], preferred_element_type=jnp.float32
        )

    def message(p):
        base = p * some * rows
        for r in range(n_seq):
            first = st2d[pl.ds(base + 2 * r, some, stride=rows), :]
            second = st2d[pl.ds(base + 2 * r + 1, some, stride=rows), :]
            stat = jnp.where(lax.rem(lane, 4) < 2, first, second)
            high = stat.astype(jnp.bfloat16).astype(jnp.float32)
            rest = stat - high
            middle = rest.astype(jnp.bfloat16).astype(jnp.float32)
            low = rest - middle
            sendb[r, p, 2] = jnp.where(
                lane < 4, high, jnp.where(lane < 8, middle, low)
            ).astype(jnp.bfloat16)
            for s in range(2):
                sendb[r, p, s] = o2d[pl.ds(base + 2 * r + s, some, stride=rows), :].astype(
                    jnp.bfloat16
                )

    def p_copy(p, step):
        return pltpu.make_async_remote_copy(
            src_ref=sendb.at[to_seq(step), p],
            dst_ref=recvb.at[me, p],
            send_sem=p_send.at[p, step - 1],
            recv_sem=p_recv.at[p, step - 1],
            device_id={"seq": to_seq(step)},
            device_id_type=MESH,
        )

    for h in range(heads + 2 * LAG):
        if h < heads:
            scores(h)
        if 0 <= h - LAG < heads:
            soften(h - LAG)
        if 0 <= h - 2 * LAG:
            weigh(h - 2 * LAG)
        if h - 2 * LAG >= 0 and (h - 2 * LAG + 1) % some == 0:
            p = (h - 2 * LAG) // some
            message(p)
            for step in range(1, n_seq):
                p_copy(p, step).start()
            recvb[me, p] = sendb[me, p]

    pair = lax.div(me, per)
    place = lax.rem(me, per)

    def merge(p):
        own_stat, own_acc = owned[p]
        stats = [own_stat]
        for j in range(n_seq):
            x = recvb[j, p, 2].astype(jnp.float32)
            x = x + pltpu.roll(x, hdim - 4, 1) + pltpu.roll(x, hdim - 8, 1)
            stats.append(x)
        highest = functools.reduce(jnp.maximum, stats)
        factors = [jnp.exp(jnp.minimum(x - highest, 0.0)) for x in stats]
        total = sum(f * pltpu.roll(x, hdim - 1, 1) for f, x in zip(factors, stats))
        inverse = 1.0 / total
        for s in range(2):
            inv = inverse[:, 2 * s : 2 * s + 1]
            acc = factors[0][:, 2 * s : 2 * s + 1] * own_acc[s]
            for j in range(n_seq):
                acc += factors[j + 1][:, 2 * s : 2 * s + 1] * recvb[j, p, s].astype(jnp.float32)
            attb[pair, place, p, s] = (acc * inv).astype(jnp.bfloat16)

    def a_copy(p, step):
        return pltpu.make_async_remote_copy(
            src_ref=attb.at[pair, place, p],
            dst_ref=attb.at[pair, place, p],
            send_sem=a_send.at[p, step - 1],
            recv_sem=a_recv.at[p, step - 1],
            device_id={"seq": to_seq(step)},
            device_id_type=MESH,
        )

    def a_wait(p, step):
        source = lax.rem(me + n_seq - step, n_seq)
        here = attb.at[lax.div(source, per), lax.rem(source, per), p]
        return pltpu.make_async_remote_copy(
            src_ref=here,
            dst_ref=here,
            send_sem=a_send.at[p, step - 1],
            recv_sem=a_recv.at[p, step - 1],
            device_id={"seq": to_seq(step)},
            device_id_type=MESH,
        )

    for p in range(PARTS):
        for step in range(1, n_seq):
            p_copy(p, step).wait_recv()
        merge(p)
        for step in range(1, n_seq):
            a_copy(p, step).start()
    for g in range(groups):
        w_copy(g).wait()

    def h_copy(c, step):
        at = slice(c * tile, (c + 1) * tile)
        return pltpu.make_async_remote_copy(
            src_ref=shares.at[to_head(step), :, at],
            dst_ref=got.at[step - 1, :, at],
            send_sem=h_send.at[c, step - 1],
            recv_sem=h_recv.at[c, step - 1],
            device_id={"head": to_head(step)},
            device_id_type=MESH,
        )

    for p in range(PARTS):
        for step in range(1, n_seq):
            a_wait(p, step).wait_recv()
        for k in range(n_head):
            for s in range(2):
                for j in range(per):
                    n = (k * 2 + s) * per + j
                    q2d[pl.ds(n * padded + p * slot, some), :] = attb[k, j, p, s].astype(
                        jnp.float32
                    )
        for h in range(some):
            x_ref[:, lanes(p * some + h)] = q2d[
                pl.ds(p * slot + h, rows, stride=padded), :
            ].astype(jnp.bfloat16)
        deep = slice(p * some * hdim, (p + 1) * some * hdim)
        for c in range(cols // tile):
            at = slice(c * tile, (c + 1) * tile)
            part = jnp.dot(x_ref[:, deep], wbuf[deep, at], preferred_element_type=jnp.float32)
            if p > 0:
                part += sofar[:, at]
            if p < PARTS - 1:
                sofar[:, at] = part
                continue
            for k in range(n_head):
                shares[k, :, at] = part[2 * per * k : 2 * per * (k + 1)].astype(jnp.bfloat16)
            for step in range(1, n_head):
                h_copy(c, step).start()

    summed = shares[mine].astype(jnp.float32)
    for step in range(1, n_head):
        for c in range(cols // tile):
            h_copy(c, step).wait_recv()
        summed += got[step - 1].astype(jnp.float32)
    for s in range(2):
        out_ref[s] = (
            res_ref[s].astype(jnp.float32) + summed[s * per : (s + 1) * per]
        ).astype(jnp.bfloat16)
    for step in range(1, n_seq):
        q_copy(step).wait_send()
        for p in range(PARTS):
            p_copy(p, step).wait_send()
            a_copy(p, step).wait_send()
    for step in range(1, n_head):
        for c in range(cols // tile):
            h_copy(c, step).wait_send()


def body(
    n_seq,
    n_head,
    queries,
    new_keys,
    new_values,
    cache_keys,
    cache_values,
    slopes,
    seg_blocks,
    request_row,
    out_weight,
    residual,
):
    heads = slopes.shape[0]
    width = queries.shape[2]
    hdim = width // heads
    tokens = cache_keys.shape[0]
    cols = out_weight.shape[1]
    assert queries.shape[1] == 1 and seg_blocks.shape[0] == n_seq
    flat = [x.reshape(2, width) for x in (queries, new_keys, new_values)]
    unit = max(u for u in (1, 2, 4) if heads % u == 0)
    tile = 256 if cols % 256 == 0 else cols
    rows = 2 * n_seq
    per = n_seq // n_head
    some = heads // PARTS
    padded = PARTS * (-(-some // 8) * 8)
    assert heads % PARTS == 0
    groups = heads // unit
    bf16, f32 = jnp.bfloat16, jnp.float32
    dma = pltpu.SemaphoreType.DMA
    vmem = pl.BlockSpec(memory_space=pltpu.VMEM)
    smem = pl.BlockSpec(memory_space=pltpu.SMEM)
    hbm = pl.BlockSpec(memory_space=pl.ANY)
    return pl.pallas_call(
        functools.partial(kernel, n_seq, n_head, heads, unit, tile),
        out_shape=jax.ShapeDtypeStruct(residual.shape, residual.dtype),
        in_specs=[vmem, vmem, vmem, smem, smem, smem, vmem, hbm, hbm, hbm],
        out_specs=vmem,
        scratch_shapes=[
            pltpu.VMEM(cache_keys.shape, bf16),
            pltpu.VMEM(cache_values.shape, bf16),
            pltpu.VMEM(out_weight.shape, bf16),
            pltpu.VMEM((n_seq, 2, width), bf16),
            pltpu.VMEM((3, 2 * heads, hdim), f32),
            pltpu.VMEM((rows, width), f32),
            pltpu.VMEM((heads * rows, tokens), f32),
            pltpu.VMEM((heads * rows, tokens), bf16),
            pltpu.VMEM((rows * padded, hdim), f32),
            pltpu.VMEM((rows, tokens), f32),
            pltpu.VMEM((heads * rows, hdim), f32),
            pltpu.VMEM((heads * rows, hdim), f32),
            pltpu.VMEM((n_seq, PARTS, 3, some, hdim), bf16),
            pltpu.VMEM((n_seq, PARTS, 3, some, hdim), bf16),
            pltpu.VMEM((n_head, per, PARTS, 2, some, hdim), bf16),
            pltpu.VMEM((rows, width), bf16),
            pltpu.VMEM((rows, cols), f32),
            pltpu.VMEM((n_head, 2 * per, cols), bf16),
            pltpu.VMEM((n_head - 1, 2 * per, cols), bf16),
            dma((groups,)),
            dma((groups,)),
            dma((groups,)),
            dma((n_seq - 1,)),
            dma((n_seq - 1,)),
            dma((PARTS, n_seq - 1)),
            dma((PARTS, n_seq - 1)),
            dma((PARTS, n_seq - 1)),
            dma((PARTS, n_seq - 1)),
            dma((cols // tile, n_head - 1)),
            dma((cols // tile, n_head - 1)),
        ],
        compiler_params=pltpu.CompilerParams(
            collective_id=0, has_side_effects=True, vmem_limit_bytes=56 << 20
        ),
    )(*flat, seg_blocks, request_row, slopes, residual, cache_keys, cache_values, out_weight)


def solution(mesh):
    in_specs = (
        P(None, "seq", "head"),
        P(None, "seq", "head"),
        P(None, "seq", "head"),
        P("seq", "head"),
        P("seq", "head"),
        P("head"),
        P(),
        P(),
        P("head", "seq"),
        P(None, "head", "seq"),
    )
    out_specs = P(None, "head", "seq")
    sizes = (mesh.shape["seq"], mesh.shape["head"])
    return jax.shard_map(
        functools.partial(body, *sizes),
        mesh=mesh,
        in_specs=in_specs,
        out_specs=out_specs,
        check_vma=False,
    )
```
